32 devices in a mesh: blk: 2 (over core), head: 16 (over z, y, x).
Axes of the slice: x: 2, y: 2, z: 4, core: 2. Of those that a mesh axis runs over, the one named last changes fastest.
Arguments:
- tokens_qkv: bfloat16 [2048, 12288], P(('blk', 'head')), may hold values from -8 to 8, as said below
- block_mask: int32 [16, 16], replicated, may hold values from 0 to 1, as said below
Outputs:
- attended: bfloat16 [2048, 4096], P(('blk', 'head'))
The draws below stay inside these ranges and needn't reach their ends.
Inputs may be any that keep to these rules, and one draw needn't show every extreme that they name: `tokens_qkv`: queries, keys and values ordered by head, then query, key, value, then the 128 entries. `block_mask`: 1 where a pair of 128-token blocks attends; a block always attends to itself whatever the entry says.
All inputs are finite; a program needn't handle non-finite values.
Results may differ from the reference program's by a relative error of at most 0.007.
Values may be sent and summed in bfloat16 or wider, within the bound.
No kernel may reach another device: no remote copies, remote signals or barrier semaphores. Data moves between devices by JAX's collectives and lax.ppermute only.
A program may use at most 64 MiB of HBM per device.

```python
import jax
import jax.numpy as jnp
from jax import lax

HEADS = 32
HD = 128
BLOCK = 128
SEQ_DEV = 1024
TOKENS = 2048
NB = 16


def draw_tokens_qkv(key, part):
    keys_list = jax.random.split(jax.random.fold_in(key, 11), 1)
    base = jnp.clip(jax.random.normal(keys_list[0], (TOKENS, HEADS, 3, HD), jnp.float32), -8.0, 8.0)
    return base.reshape(TOKENS, 3 * HEADS * HD).astype(jnp.bfloat16)


def draw_block_mask(key, part):
    first, second = jax.random.split(jax.random.fold_in(key, 23))
    groups = TOKENS // SEQ_DEV
    per_group = SEQ_DEV // BLOCK
    level = jax.random.randint(first, (groups, groups), 1, 8)
    level = jnp.repeat(jnp.repeat(level, per_group, axis=0), per_group, axis=1)
    rolled = jax.random.randint(second, (NB, NB), 0, 8)
    result = (rolled < level).astype(jnp.int32)
    result = result.at[0, 1].set(0).at[1, 0].set(1)
    return result


def setup_inputs(seed: int = 0) -> dict:
    streams_of = jax.random.split(jax.random.key(seed), 3)
    tokens_qkv = draw_tokens_qkv(jax.random.fold_in(streams_of[2], 71), 0)
    block_mask = draw_block_mask(jax.random.fold_in(streams_of[2], 71), 0)
    return dict(tokens_qkv=tokens_qkv, block_mask=block_mask)


def reference(tokens_qkv, block_mask):
    packed = tokens_qkv.reshape(TOKENS, HEADS, 3, HD)
    by_heads = jnp.transpose(packed, (1, 2, 0, 3))
    blocks = TOKENS // BLOCK
    allowed = (block_mask == 1) | jnp.eye(blocks, dtype=bool)
    allowed = jnp.broadcast_to(allowed[:, None, :, None], (blocks, BLOCK, blocks, BLOCK)).reshape(TOKENS, TOKENS)
    factor_scale = HD ** -0.5

    def one_head(triple):
        scores = jnp.dot(triple[0], triple[1].T, preferred_element_type=jnp.float32) * factor_scale
        scores = jnp.where(allowed, scores, -1e30)
        largest = jnp.max(scores, axis=1, keepdims=True)
        weights = jnp.where(allowed, jnp.exp(scores - largest), 0.0)
        totals = jnp.sum(weights, axis=1, keepdims=True)
        summed = jnp.dot(weights.astype(jnp.bfloat16), triple[2], preferred_element_type=jnp.float32)
        return (summed / totals).astype(jnp.bfloat16)

    outputs = lax.map(one_head, by_heads)
    return jnp.transpose(outputs, (1, 0, 2)).reshape(TOKENS, HEADS * HD)
```

```python
import functools
import math

import jax
import jax.numpy as jnp
from jax import lax
from jax.experimental import pallas as pl
from jax.experimental.pallas import tpu as pltpu
from jax.sharding import PartitionSpec as P

HD = 128
BLOCK = 128
NEGATIVE = -1e30


VMEM = pl.BlockSpec(memory_space=pltpu.VMEM)
SMEM = pl.BlockSpec(memory_space=pltpu.SMEM)
FACTOR = HD**-0.5 * math.log2(math.e)


def attend_kernel(n, cycle, mask_ref, *refs):
    pieces, (out_ref, q_ref, s_ref) = refs[:-3], refs[-3:]
    per_shard = len(pieces) // cycle
    own_pieces = pieces[:per_shard]
    rows = out_ref.shape[1]
    size = n * rows
    heads = out_ref.shape[2] // HD
    blocks = size // BLOCK
    per = BLOCK // rows
    me, own = lax.axis_index("head"), lax.axis_index("blk")
    turn = me // per
    columns = [((own - hop) % cycle) * blocks + jnp.bitwise_xor(turn, j) for hop in range(cycle) for j in range(blocks)]

    def part_of(which, h, part):
        base = (3 * h + part) * HD
        return jnp.concatenate([piece[:, base : base + HD] for piece in which], axis=0)

    for h in range(heads):
        for p, piece in enumerate(own_pieces):
            at = pl.ds(p * piece.shape[0], piece.shape[0])
            q_ref[h, at, :] = piece[:, 3 * h * HD : (3 * h + 1) * HD]

    unroll = math.lcm(2, heads)
    units = heads * blocks
    keys = cycle * size

    def score(tile, h, slot):
        at = pl.ds(pl.multiple_of(tile * BLOCK, BLOCK), BLOCK)
        s_ref[slot] = lax.dot_general(
            q_ref[h, at, :], part_of(pieces, h, 1), (((1,), (1,)), ((), ())),
            preferred_element_type=jnp.float32,
        )

    def finish(tile, h, slot):
        row = own * blocks + jnp.bitwise_xor(turn, tile)
        top = None
        for j in range(cycle * blocks):
            live = (mask_ref[row, columns[j]] == 1) | (row == columns[j])
            part = s_ref[slot, :, j * BLOCK : (j + 1) * BLOCK] * FACTOR + jnp.where(live, 0.0, NEGATIVE)
            s_ref[slot, :, j * BLOCK : (j + 1) * BLOCK] = part
            top = part if top is None else jnp.maximum(top, part)
        top = jnp.broadcast_to(jnp.max(top, axis=1, keepdims=True), top.shape)
        weights, total = [], None
        for j in range(cycle * blocks):
            w = jnp.exp2(s_ref[slot, :, j * BLOCK : (j + 1) * BLOCK] - top)
            total = w if total is None else total + w
            weights.append(w.astype(jnp.bfloat16))
        value = jnp.dot(
            jnp.concatenate(weights, axis=1), part_of(pieces, h, 2), preferred_element_type=jnp.float32
        )
        value = (value / jnp.sum(total, axis=1, keepdims=True)).astype(jnp.bfloat16)
        for part in range(per):
            peer = jnp.bitwise_xor(tile * per + part, me)
            out_ref[peer, :, h * HD : (h + 1) * HD] = value[part * rows : (part + 1) * rows]

    score(0, 0, 0)

    @pl.loop(0, units // unroll)
    def _(p):
        for j in range(unroll):
            tile, h = p * (unroll // heads) + j // heads, j % heads
            after = p * (unroll // heads) + (j + 1) // heads
            score(jnp.minimum(after, blocks - 1), (j + 1) % heads, (j + 1) % 2)
            finish(tile, h, j % 2)


def on_device(tokens_qkv, block_mask):
    n, cycle = lax.axis_size("head"), lax.axis_size("blk")
    me = lax.axis_index("head")
    rows = tokens_qkv.shape[0]
    width = tokens_qkv.shape[1] // n
    heads = width // (3 * HD)
    size = rows * n
    along = [(i, (i + 1) % cycle) for i in range(cycle)]

    slots = {0: lax.dynamic_slice(tokens_qkv, (0, me * width), (rows, width))}
    for k in sorted(range(1, n), key=lambda k: (-(k >> 2), k), reverse=True):
        block = lax.dynamic_slice(tokens_qkv, (0, (me ^ k) * width), (rows, width))
        slots[k] = lax.ppermute(block, "head", [(i, i ^ k) for i in range(n)])

    pieces = [slots[k] for k in range(n)]
    if cycle > 2:
        pieces = [jnp.concatenate(pieces, axis=0)]
    shards = [pieces]
    for _ in range(1, cycle):
        shards.append([lax.ppermute(piece, "blk", along) for piece in shards[-1]])

    keys = cycle * size
    result = pl.pallas_call(
        functools.partial(attend_kernel, n, cycle),
        out_shape=jax.ShapeDtypeStruct((n, rows, heads * HD), jnp.bfloat16),
        in_specs=[SMEM] + [VMEM] * (len(pieces) * cycle),
        out_specs=VMEM,
        scratch_shapes=[
            pltpu.VMEM((heads, size, HD), jnp.bfloat16),
            pltpu.VMEM((2, BLOCK, keys), jnp.float32),
        ],
        cost_estimate=pl.CostEstimate(
            flops=4 * heads * size * keys * HD,
            bytes_accessed=6 * heads * keys * HD,
            transcendentals=heads * size * keys,
        ),
        name="attend",
    )(block_mask, *(piece for shard in shards for piece in shard))

    back = lax.all_to_all(result, "head", split_axis=0, concat_axis=0, tiled=True)
    return back.transpose(1, 0, 2).reshape(rows, n * heads * HD)


def solution(mesh):
    return jax.shard_map(
        on_device,
        mesh=mesh,
        in_specs=(P(("blk", "head"), None), P()),
        out_specs=P(("blk", "head"), None),
        check_vma=False,
    )
```
